512 devices in a mesh: node: 4 (over x), gx: 16 (over z, y_hi), gy: 8 (over y_lo, core).
Axes of the slice: x: 4, y: 8 (y_hi: 2, y_lo: 4; y = y_hi * 4 + y_lo), z: 8, core: 2. Of those that a mesh axis runs over, the one named last changes fastest.
Arguments:
- initial: float32 [5, 192, 128, 128], P(None, 'gx', 'gy'), may hold values from -8 to 50, as said below
- guesses: float32 [4, 5, 192, 128, 128], P('node', None, 'gx', 'gy'), may hold values from -8 to 50, as said below
Outputs:
- node_states: float32 [4, 5, 192, 128, 128], P('node', None, 'gx', 'gy')
The draws below stay inside these ranges and needn't reach their ends.
Inputs may be any that keep to these rules, and one draw needn't show every extreme that they name: `initial`: each cell holds density, three momenta and total energy of a gas with ratio of heats 1.4: density 0.5 to 2.5, pressure 0.3 to 9, velocity components at most 3 in magnitude. `guesses`: each cell of each node holds density, three momenta and total energy of a gas with ratio of heats 1.4: density 0.5 to 2.5, pressure 0.3 to 9, velocity components at most 3 in magnitude.
All inputs are finite; a program needn't handle non-finite values.
Results may differ from the reference program's by a relative error of at most 0.0001.
Values sent between devices are 32-bit elements; how exact they have to be, the bound alone decides.
A program may use at most 64 MiB of HBM per device.

```python
import math
import jax
import jax.numpy as jnp
from jax import lax

NODES = 4
SWEEPS = 2
NX = 192
NY = 128
NZ = 128


def make_states(base_key, count):
    subkeys = jax.random.split(base_key, 3)
    grid_shape = (count, NX, NY, NZ)
    position = jnp.arange(NX, dtype=jnp.float32) / max(NX - 1, 1)
    rising = (9.0 ** position)[None, :, None, None]
    density = jnp.exp(jax.random.uniform(subkeys[0], grid_shape, jnp.float32, math.log(0.5), math.log(2.0)))
    velocity = jnp.clip(jax.random.normal(subkeys[1], (3,) + grid_shape, jnp.float32), -3.0, 3.0)
    base_pressure = jnp.exp(jax.random.uniform(subkeys[2], grid_shape, jnp.float32, math.log(0.3), 0.0))
    pressure = base_pressure * rising
    momentum = density[None] * velocity
    energy = pressure / 0.4 + 0.5 * density * jnp.sum(velocity * velocity, axis=0)
    return jnp.stack([density, momentum[0], momentum[1], momentum[2], energy], axis=1)


def draw_initial(key, part):
    return make_states(jax.random.fold_in(key, 11), 1)[0]


def draw_guesses(key, part):
    return make_states(jax.random.fold_in(key, 23), NODES)


def setup_inputs(seed: int = 0) -> dict:
    arg_keys = jax.random.split(jax.random.key(seed), 3)
    initial = draw_initial(jax.random.fold_in(arg_keys[2], 71), 0)
    guesses = draw_guesses(jax.random.fold_in(arg_keys[2], 71), 0)
    return dict(initial=initial, guesses=guesses)


heat_ratio = 1.4
step_size = 0.025
density_floor = 0.5
pressure_floor = 0.25
epsilon = 1e-06
radau_weights = [[0.112999479323156, -0.040309220723522, 0.025802377420336, -0.009904676507266], [0.2343839957474, 0.206892573935359, -0.047857128048541, 0.016047422806516], [0.21668178462325, 0.406123263867373, 0.189036518170056, -0.024182104899833], [0.220462211176768, 0.388193468843172, 0.32884431998006, 0.0625]]

def primitives(fields):
    density = jnp.maximum(fields[0], density_floor)
    velocity = fields[1:4] / density
    pressure = jnp.maximum(0.4 * (fields[4] - 0.5 * lax.optimization_barrier(jnp.sum(fields[1:4] * velocity, axis=0))), pressure_floor)
    return (density, velocity, pressure)

def wave_speeds(fields):
    density, velocity, pressure = primitives(fields)
    sound = jnp.sqrt(heat_ratio * pressure / density)
    return tuple((jnp.max(jnp.abs(velocity[direction]) + sound) for direction in range(3)))

def reconstruct(first, second, third, fourth, fifth):
    cand_zero = (2.0 * first - 7.0 * second + 11.0 * third) / 6.0
    cand_one = (-second + 5.0 * third + 2.0 * fourth) / 6.0
    cand_two = (2.0 * third + 5.0 * fourth - fifth) / 6.0
    smooth_zero = 13.0 / 12.0 * (first - 2.0 * second + third) ** 2 + 0.25 * (first - 4.0 * second + 3.0 * third) ** 2
    smooth_one = 13.0 / 12.0 * (second - 2.0 * third + fourth) ** 2 + 0.25 * (second - fourth) ** 2
    smooth_two = 13.0 / 12.0 * (third - 2.0 * fourth + fifth) ** 2 + 0.25 * (3.0 * third - 4.0 * fourth + fifth) ** 2
    weight_zero = 0.1 / (epsilon + smooth_zero) ** 2
    weight_one = 0.6 / (epsilon + smooth_one) ** 2
    weight_two = 0.3 / (epsilon + smooth_two) ** 2
    return (weight_zero * cand_zero + weight_one * cand_one + weight_two * cand_two) / (weight_zero + weight_one + weight_two)

def flux_along(extended, spatial_axis, alpha):
    direction = spatial_axis - 1
    density, velocity, pressure = primitives(extended)
    speed = velocity[direction]
    components = [extended[direction + 1], extended[1] * speed, extended[2] * speed, extended[3] * speed, (extended[4] + pressure) * speed]
    components[direction + 1] = components[direction + 1] + pressure
    fluxes = jnp.stack(components)
    right_going = 0.5 * (fluxes + alpha * extended)
    left_going = 0.5 * (fluxes - alpha * extended)
    length = extended.shape[spatial_axis] - 6

    def window(values, begin):
        return lax.slice_in_dim(values, begin, begin + length + 1, axis=spatial_axis)
    interface = reconstruct(window(right_going, 0), window(right_going, 1), window(right_going, 2), window(right_going, 3), window(right_going, 4))
    interface = interface + reconstruct(window(left_going, 5), window(left_going, 4), window(left_going, 3), window(left_going, 2), window(left_going, 1))
    return lax.slice_in_dim(interface, 0, length, axis=spatial_axis) - lax.slice_in_dim(interface, 1, length + 1, axis=spatial_axis)

def wrapped(fields, spatial_axis):
    size_here = fields.shape[spatial_axis]
    lower = lax.slice_in_dim(fields, size_here - 3, size_here, axis=spatial_axis)
    upper = lax.slice_in_dim(fields, 0, 3, axis=spatial_axis)
    return jnp.concatenate([lower, fields, upper], axis=spatial_axis)

def evaluate(fields):
    alphas = wave_speeds(fields)
    summed = flux_along(wrapped(fields, 1), 1, alphas[0])
    summed = summed + flux_along(wrapped(fields, 2), 2, alphas[1])
    summed = summed + flux_along(wrapped(fields, 3), 3, alphas[2])
    return summed

def reference(initial, guesses):
    current = [guesses[node] for node in range(NODES)]
    for sweep_index in range(SWEEPS):
        rates = [evaluate(fields) for fields in current]
        updated = []
        for target in range(NODES):
            combined = jnp.zeros_like(initial)
            for source in range(NODES):
                combined = combined + radau_weights[target][source] * rates[source]
            updated.append(initial + step_size * combined)
        current = updated
    return jnp.stack(current)
```

```python
import functools

import jax
import jax.numpy as jnp
from jax import lax
from jax.experimental import pallas as pl
from jax.experimental.pallas import tpu as pltpu
from jax.sharding import PartitionSpec as P

SWEEPS = 2
SCALE = 1.0 / 64.0

heat_ratio = 1.4
step_size = 0.025
density_floor = 0.5
pressure_floor = 0.25
epsilon = 1e-06
radau_weights = [
    [0.112999479323156, -0.040309220723522, 0.025802377420336, -0.009904676507266],
    [0.2343839957474, 0.206892573935359, -0.047857128048541, 0.016047422806516],
    [0.21668178462325, 0.406123263867373, 0.189036518170056, -0.024182104899833],
    [0.220462211176768, 0.388193468843172, 0.32884431998006, 0.0625],
]
MESH = pl.DeviceIdType.MESH
EPS = epsilon * 4.0 * SCALE * SCALE
NX, NY, LANES = 12, 16, 128
CHUNKS = ((3, 3), (6, 3), (0, 3), (9, 3))
YROWS = 40


def primitives(u):
    density = jnp.maximum(u[0], density_floor * SCALE)
    inverse = 1.0 / density
    velocity = [u[k] * inverse for k in (1, 2, 3)]
    kinetic = u[1] * velocity[0] + u[2] * velocity[1] + u[3] * velocity[2]
    pressure = jnp.maximum(0.4 * (u[4] - 0.5 * kinetic), pressure_floor * SCALE)
    return inverse, velocity, pressure


def flux(u, velocity, pressure, k):
    speed = velocity[k]
    parts = [u[k + 1], u[1] * speed, u[2] * speed, u[3] * speed, (u[4] + pressure) * speed]
    parts[k + 1] = parts[k + 1] + pressure
    return parts


class Line:
    def __init__(self, cells):
        self.cells = cells
        self.made = {}

    def get(self, name, i):
        key = (name, i)
        if key not in self.made:
            self.made[key] = getattr(self, "make_" + name)(i)
        return self.made[key]

    def g(self, i):
        return self.cells[i]

    def make_d(self, i):
        return self.cells[i + 1] - self.cells[i]

    def make_e(self, i):
        return self.get("d", i + 1) - self.get("d", i)

    def make_t(self, i):
        return self.get("e", i + 1) - self.get("e", i)

    def make_p(self, i):
        d = self.get("d", i)
        return d * d + EPS

    def make_k(self, i):
        e = self.get("e", i)
        return (4.0 / 3.0) * (e * e)

    def make_x(self, i):
        return self.get("e", i) * self.get("d", i)

    def make_q(self, i):
        return self.get("k", i) + self.get("p", i)

    def make_l(self, i):
        s = self.get("k", i) + self.get("e", i) * self.get("d", i + 1) + self.get("p", i + 1)
        return s * s

    def make_m(self, i):
        s = self.get("q", i) + self.get("x", i)
        return s * s

    def make_r(self, i):
        s = self.get("q", i) - self.get("x", i)
        return s * s


def correction(s0, s1, s2, t0, t2):
    a = 3.0 * s0
    r2 = s2 + s2
    total = s1 * s2 + a * (r2 + s1)
    return (s1 * (1.0 / total)) * (r2 * t0 + a * t2)


def interface(plus, minus, i):
    cp = correction(
        plus.get("l", i - 2), plus.get("m", i - 1), plus.get("r", i),
        plus.get("t", i - 2), plus.get("t", i - 1),
    )
    cm = correction(
        minus.get("r", i + 1), minus.get("m", i), minus.get("l", i - 1),
        minus.get("t", i), minus.get("t", i - 1),
    )
    near = plus.get("d", i) - minus.get("d", i)
    far = plus.get("d", i - 1) - minus.get("d", i + 1)
    return (plus.g(i) + minus.g(i + 1)) + (1.0 / 6.0) * ((near + near) + far + (cm - cp))


def pick(index, values):
    out = jnp.float32(values[-1])
    for k in range(len(values) - 2, -1, -1):
        out = jnp.where(index == k, jnp.float32(values[k]), out)
    return out


def kernel(
    sizes, init_hbm, guess_hbm, out_hbm,
    w, fx, fy, fz, gs, hs, hx, rate, r1, s2, r2, init, stage,
    ysend, yrecv, fyp, part, amsg, ar1, amid, ar2, alpha,
    load_sem, out_sem, xs_sem, xr_sem, ys_sem, yr_sem,
    a1s_sem, a1r_sem, a2s_sem, a2r_sem, e1s_sem, e1r_sem, e2s_sem, e2r_sem,
):
    n_gx, n_gy = sizes
    n_z, n_y = n_gx // 2, 2 * n_gy
    node, gx, gy = lax.axis_index("node"), lax.axis_index("gx"), lax.axis_index("gy")
    mate_a = node + 1 - 2 * lax.rem(node, 2)
    mate_b = 3 - node
    z, hi = gx // 2, lax.rem(gx, 2)
    y = hi * n_gy + gy

    def y_peer(step):
        other = lax.rem(y + step, n_y)
        return {"gx": z * 2 + other // n_gy, "gy": lax.rem(other, n_gy)}

    def z_peer(step):
        return {"gx": lax.rem(z + step, n_z) * 2 + hi}

    up_x = {"gx": lax.rem(gx + 1, n_gx)}
    down_x = {"gx": lax.rem(gx + n_gx - 1, n_gx)}
    up_y = {"gy": lax.rem(gy + 1, n_gy)}
    down_y = {"gy": lax.rem(gy + n_gy - 1, n_gy)}
    first_mates = ({"node": mate_a}, {"node": mate_b})
    second_mates = ({"node": mate_b}, {"node": mate_a})

    load_init = pltpu.make_async_copy(init_hbm, init, load_sem.at[0])
    load_guess = pltpu.make_async_copy(guess_hbm.at[0], stage, load_sem.at[1])
    load_guess.start()
    load_init.start()

    barrier = pltpu.get_barrier_semaphore()
    greeted = [y_peer(k) for k in range(1, n_y)] + [z_peer(k) for k in range(1, n_z)]
    greeted += [up_x, down_x, {"node": mate_a}, {"node": mate_b}]
    for peer in greeted:
        pl.semaphore_signal(barrier, inc=1, device_id=peer, device_id_type=MESH)

    def entry(f):
        return pick(node, [0.5 * step_size * f(m, m + 1 - 2 * (m % 2), 3 - m) for m in range(4)])

    table = radau_weights
    own = entry(lambda m, a, b: table[m][m])
    got = (entry(lambda m, a, b: table[m][a]), entry(lambda m, a, b: table[m][b]))
    give_own = (entry(lambda m, a, b: table[b][m]), entry(lambda m, a, b: table[a][m]))
    give_got = (entry(lambda m, a, b: table[b][a]), entry(lambda m, a, b: table[a][b]))

    def rows(h):
        return slice(8 + 8 * h, 16 + 8 * h)

    def half(h):
        return slice(8 * h, 8 * h + 8)

    def take_plane(s, p, fields):
        best = [part[k] for k in range(3)]
        for h in range(2):
            u = fields[h]
            inverse, velocity, pressure = primitives(u)
            sound = jnp.sqrt(heat_ratio * pressure * inverse)
            for k in range(3):
                best[k] = jnp.maximum(best[k], jnp.abs(velocity[k]) + sound)
            f0, f1, f2 = (flux(u, velocity, pressure, k) for k in range(3))
            for c in range(5):
                w[s, c, p + 3, rows(h), :] = u[c]
                fx[c, p + 3, half(h), :] = f0[c]
                fy[c, p, rows(h), :] = f1[c]
                fz[c, p, half(h), :] = f2[c]
        for k in range(3):
            part[k] = best[k]

    for k in range(3):
        part[k] = jnp.zeros((8, LANES), jnp.float32)
    load_guess.wait()

    def first(p, _):
        take_plane(0, p, [[stage[c, p, half(h), :] * SCALE for c in range(5)] for h in range(2)])
        return 0

    lax.fori_loop(0, NX, first, 0)
    load_init.wait()
    pl.semaphore_wait(barrier, len(greeted))

    def x_halo(s):
        low = pltpu.make_async_remote_copy(
            src_ref=w.at[s, :, pl.ds(3, 3), pl.ds(8, 16), :], dst_ref=w.at[s, :, pl.ds(15, 3), pl.ds(8, 16), :],
            send_sem=xs_sem.at[0], recv_sem=xr_sem.at[s, 0], device_id=down_x, device_id_type=MESH)
        high = pltpu.make_async_remote_copy(
            src_ref=w.at[s, :, pl.ds(12, 3), pl.ds(8, 16), :], dst_ref=w.at[s, :, pl.ds(0, 3), pl.ds(8, 16), :],
            send_sem=xs_sem.at[1], recv_sem=xr_sem.at[s, 1], device_id=up_x, device_id_type=MESH)
        return low, high

    def y_halo(s):
        low = pltpu.make_async_remote_copy(
            src_ref=ysend.at[0], dst_ref=yrecv.at[s, 1],
            send_sem=ys_sem.at[0], recv_sem=yr_sem.at[s, 1], device_id=down_y, device_id_type=MESH)
        high = pltpu.make_async_remote_copy(
            src_ref=ysend.at[1], dst_ref=yrecv.at[s, 0],
            send_sem=ys_sem.at[1], recv_sem=yr_sem.at[s, 0], device_id=up_y, device_id_type=MESH)
        return low, high

    def swap(s, h, chunk, second):
        start, count = CHUNKS[chunk]
        span = pl.ds(start, count)
        return pltpu.make_async_remote_copy(
            src_ref=(s2 if second else rate).at[h, span], dst_ref=(r2 if second else r1).at[s, h, span],
            send_sem=(e2s_sem if second else e1s_sem).at[h, chunk],
            recv_sem=(e2r_sem if second else e1r_sem).at[s, h, chunk],
            device_id=(second_mates if second else first_mates)[h], device_id_type=MESH)

    def x_pass(s, cells, faces, planes, saved_in, saved_out):
        def body(c, _):
            a = alpha[0]
            for h in range(2):
                up, down = {}, {}
                for i in cells:
                    f = fx[c, i, half(h), :]
                    au = a * w[s, c, i, rows(h), :]
                    up[i] = f + au
                    down[i] = f - au
                up, down = Line(up), Line(down)
                flows = {}
                for i, slot in saved_in:
                    flows[i] = hx[slot, h, c]
                for i in faces:
                    flows[i] = interface(up, down, i - 1)
                for i, slot in saved_out:
                    hx[slot, h, c] = flows[i]
                for i in planes:
                    rate[h, i - 3, c] = flows[i] - flows[i + 1]
            return 0

        lax.fori_loop(0, 5, body, 0)

    def yz_plane(s, p):
        a1 = alpha[1]
        a2 = alpha[2]
        for c in range(5):
            for j in range(4):
                tile = slice(8 * j, 8 * j + 8)
                f = fy[c, p, tile, :]
                au = a1 * w[s, c, p + 3, tile, :]
                gs[0, c, tile, :] = f + au
                gs[1, c, tile, :] = f - au
        for c in range(5):
            for j in range(3):
                base = 8 + 8 * j
                up = Line({i: gs[0, c, base - 1 + i : base + 7 + i, :] for i in range(-2, 3)})
                down = Line({i: gs[1, c, base - 1 + i : base + 7 + i, :] for i in range(-1, 4)})
                hs[c, 8 * j : 8 * j + 8, :] = interface(up, down, 0)
        for c in range(5):
            for h in range(2):
                f = fz[c, p, half(h), :]
                au = a2 * w[s, c, p + 3, rows(h), :]
                right, left = f + au, f - au
                up = Line({i: right if i == 0 else pltpu.roll(right, (-i) % LANES, 1) for i in range(-2, 3)})
                down = Line({i: left if i == 0 else pltpu.roll(left, (-i) % LANES, 1) for i in range(-1, 4)})
                flow = interface(up, down, 0)
                along_z = pltpu.roll(flow, 1, 1) - flow
                along_y = hs[c, half(h), :] - hs[c, 8 * h + 1 : 8 * h + 9, :]
                rate[h, p, c] = rate[h, p, c] + (along_y + along_z)

    def combine(s, chunk):
        start, count = CHUNKS[chunk]
        for h in range(2):
            swap(s, h, chunk, False).wait_recv()

            def body(p, _, h=h):
                for c in range(5):
                    s2[h, p, c] = give_own[h] * rate[h, p, c] + give_got[h] * r1[s, h, p, c]
                return 0

            lax.fori_loop(start, start + count, body, 0)
            swap(s, h, chunk, True).start()

    def finish(s, chunk):
        start, count = CHUNKS[chunk]
        for h in range(2):
            swap(s, h, chunk, True).wait_recv()

        def updated(p):
            return [
                [
                    init[c, p, half(h), :] * SCALE
                    + (own * rate[h, p, c] + (got[h] * r1[s, h, p, c] + r2[s, h, p, c]))
                    for c in range(5)
                ]
                for h in range(2)
            ]

        @pl.when(s < SWEEPS - 1)
        def _():
            def body(p, _):
                take_plane(s + 1, p, updated(p))
                return 0

            lax.fori_loop(start, start + count, body, 0)

        @pl.when(s == SWEEPS - 1)
        def _():
            def body(p, _):
                fields = updated(p)
                for h in range(2):
                    for c in range(5):
                        stage[c, p, half(h), :] = fields[h][c] * (1.0 / SCALE)
                return 0

            lax.fori_loop(start, start + count, body, 0)

    def whole(ref, sem):
        return pltpu.make_async_copy(ref, ref, sem)

    def sweep(s, _):
        for k in range(3):
            amsg[k : k + 1, :] = jnp.max(part[k], axis=0, keepdims=True)
        for k in range(1, n_y):
            pltpu.make_async_remote_copy(
                src_ref=amsg, dst_ref=ar1.at[s, k - 1], send_sem=a1s_sem, recv_sem=a1r_sem.at[s],
                device_id=y_peer(k), device_id_type=MESH).start()
        for copy in x_halo(s):
            copy.start()
        for c in range(5):
            for p in range(NX):
                ysend[0, c, 3 * p : 3 * p + 3, :] = w[s, c, p + 3, 8:11, :]
                ysend[1, c, 3 * p : 3 * p + 3, :] = w[s, c, p + 3, 21:24, :]
        for copy in y_halo(s):
            copy.start()
        whole(ar1.at[s], a1r_sem.at[s]).wait()
        best = amsg[...]
        for k in range(n_y - 1):
            best = jnp.maximum(best, ar1[s, k])
        amid[...] = best
        for k in range(1, n_z):
            pltpu.make_async_remote_copy(
                src_ref=amid, dst_ref=ar2.at[s, k - 1], send_sem=a2s_sem, recv_sem=a2r_sem.at[s],
                device_id=z_peer(k), device_id_type=MESH).start()

        for side, copy in ((1, y_halo(s)[0]), (0, y_halo(s)[1])):
            copy.wait_recv()
            for j in range(5):
                tile = slice(8 * j, 8 * j + 8)
                u = [yrecv[s, side, c, tile, :] for c in range(5)]
                _, velocity, pressure = primitives(u)
                parts = flux(u, velocity, pressure, 1)
                for c in range(5):
                    fyp[side, c, tile, :] = parts[c]
            at = slice(5, 8) if side == 0 else slice(24, 27)
            for c in range(5):
                for p in range(NX):
                    w[s, c, p + 3, at, :] = yrecv[s, side, c, 3 * p : 3 * p + 3, :]
                    fy[c, p, at, :] = fyp[side, c, 3 * p : 3 * p + 3, :]

        if n_z > 1:
            whole(ar2.at[s], a2r_sem.at[s]).wait()
            best = amid[...]
            for k in range(n_z - 1):
                best = jnp.maximum(best, ar2[s, k])
        for k in range(3):
            top = jnp.max(best[k : k + 1, :], axis=1, keepdims=True)
            alpha[k] = jnp.broadcast_to(top, (8, LANES))
            part[k] = jnp.zeros((8, LANES), jnp.float32)

        x_pass(s, range(3, 15), range(6, 13), range(6, 12), (), ((6, 0), (12, 1)))

        def run(chunk):
            start, count = CHUNKS[chunk]

            def body(p, _):
                yz_plane(s, p)
                return 0

            lax.fori_loop(start, start + count, body, 0)
            for h in range(2):
                swap(s, h, chunk, False).start()

        run(0)
        run(1)
        low, high = x_halo(s)
        low.wait_recv()
        high.wait_recv()

        def halo_plane(i, _):
            i = jnp.where(i < 3, i, i + 12)
            for h in range(2):
                u = [w[s, c, i, rows(h), :] for c in range(5)]
                _, velocity, pressure = primitives(u)
                parts = flux(u, velocity, pressure, 0)
                for c in range(5):
                    fx[c, i, half(h), :] = parts[c]
            return 0

        lax.fori_loop(0, 6, halo_plane, 0)
        x_pass(s, range(0, 8), range(3, 6), range(3, 6), ((6, 0),), ())
        x_pass(s, range(10, 18), range(13, 16), range(12, 15), ((12, 1),), ())
        combine(s, 0)
        run(2)
        combine(s, 1)
        run(3)
        low.wait_send()
        high.wait_send()
        for copy in y_halo(s):
            copy.wait_send()
        whole(ar1.at[s], a1s_sem).wait()
        if n_z > 1:
            whole(ar2.at[s], a2s_sem).wait()
        finish(s, 0)
        combine(s, 2)
        finish(s, 1)
        combine(s, 3)
        finish(s, 2)
        finish(s, 3)
        for chunk in range(len(CHUNKS)):
            for h in range(2):
                swap(s, h, chunk, False).wait_send()
                swap(s, h, chunk, True).wait_send()
        return 0

    lax.fori_loop(0, SWEEPS, sweep, 0)
    store = pltpu.make_async_copy(stage, out_hbm.at[0], out_sem)
    store.start()
    store.wait()


def call(sizes, initial, guesses):
    n_z, n_y = sizes[0] // 2, 2 * sizes[1]
    f32 = jnp.float32
    dma = pltpu.SemaphoreType.DMA
    chunks = len(CHUNKS)
    tile = (8, LANES)

    def vm(*shape):
        return pltpu.VMEM(shape, f32)

    return pl.pallas_call(
        functools.partial(kernel, sizes),
        out_shape=jax.ShapeDtypeStruct(guesses.shape, f32),
        in_specs=[pl.BlockSpec(memory_space=pl.ANY)] * 2,
        out_specs=pl.BlockSpec(memory_space=pl.ANY),
        scratch_shapes=[
            vm(SWEEPS, 5, NX + 6, 32, LANES),
            vm(5, NX + 6, NY, LANES),
            vm(5, NX, 32, LANES),
            vm(5, NX, NY, LANES),
            vm(2, 5, 40, LANES),
            vm(5, 24, LANES),
            vm(2, 2, 5, *tile),
            vm(2, NX, 5, *tile),
            vm(SWEEPS, 2, NX, 5, *tile),
            vm(2, NX, 5, *tile),
            vm(SWEEPS, 2, NX, 5, *tile),
            vm(5, NX, NY, LANES),
            vm(5, NX, NY, LANES),
            vm(2, 5, YROWS, LANES),
            vm(SWEEPS, 2, 5, YROWS, LANES),
            vm(2, 5, YROWS, LANES),
            vm(3, *tile),
            vm(*tile),
            vm(SWEEPS, n_y - 1, *tile),
            vm(*tile),
            vm(SWEEPS, max(n_z - 1, 1), *tile),
            vm(3, *tile),
            dma((2,)), dma,
            dma((2,)), dma((SWEEPS, 2)), dma((2,)), dma((SWEEPS, 2)),
            dma, dma((SWEEPS,)), dma, dma((SWEEPS,)),
            dma((2, chunks)), dma((SWEEPS, 2, chunks)), dma((2, chunks)), dma((SWEEPS, 2, chunks)),
        ],
        compiler_params=pltpu.CompilerParams(
            collective_id=0, has_side_effects=True, vmem_limit_bytes=40 << 20
        ),
    )(initial, guesses)


def solution(mesh):
    sizes = (mesh.shape["gx"], mesh.shape["gy"])
    placed = (P(None, "gx", "gy", None), P("node", None, "gx", "gy", None))
    return jax.shard_map(
        functools.partial(call, sizes),
        mesh=mesh,
        in_specs=placed,
        out_specs=P("node", None, "gx", "gy", None),
        check_vma=False,
    )
```

```python
import functools

import jax
import jax.numpy as jnp
from jax import lax
from jax.experimental import pallas as pl
from jax.experimental.pallas import tpu as pltpu
from jax.sharding import PartitionSpec as P

SWEEPS = 2
SCALE = 1.0 / 64.0

heat_ratio = 1.4
step_size = 0.025
density_floor = 0.5
pressure_floor = 0.25
epsilon = 1e-06
radau_weights = [
    [0.112999479323156, -0.040309220723522, 0.025802377420336, -0.009904676507266],
    [0.2343839957474, 0.206892573935359, -0.047857128048541, 0.016047422806516],
    [0.21668178462325, 0.406123263867373, 0.189036518170056, -0.024182104899833],
    [0.220462211176768, 0.388193468843172, 0.32884431998006, 0.0625],
]
MESH = pl.DeviceIdType.MESH
EPS = epsilon * 4.0 * SCALE * SCALE
NX, NY, LANES = 12, 16, 128
CHUNKS = ((3, 3), (6, 3), (0, 3), (9, 3))
YROWS = 40


def primitives(u):
    density = jnp.maximum(u[0], density_floor * SCALE)
    inverse = 1.0 / density
    velocity = [u[k] * inverse for k in (1, 2, 3)]
    kinetic = u[1] * velocity[0] + u[2] * velocity[1] + u[3] * velocity[2]
    pressure = jnp.maximum(0.4 * (u[4] - 0.5 * kinetic), pressure_floor * SCALE)
    return inverse, velocity, pressure


def flux(u, velocity, pressure, k):
    speed = velocity[k]
    parts = [u[k + 1], u[1] * speed, u[2] * speed, u[3] * speed, (u[4] + pressure) * speed]
    parts[k + 1] = parts[k + 1] + pressure
    return parts


class Line:
    def __init__(self, cells):
        self.cells = cells
        self.made = {}

    def get(self, name, i):
        key = (name, i)
        if key not in self.made:
            self.made[key] = getattr(self, "make_" + name)(i)
        return self.made[key]

    def g(self, i):
        return self.cells[i]

    def make_d(self, i):
        return self.cells[i + 1] - self.cells[i]

    def make_e(self, i):
        return self.get("d", i + 1) - self.get("d", i)

    def make_t(self, i):
        return self.get("e", i + 1) - self.get("e", i)

    def make_p(self, i):
        d = self.get("d", i)
        return d * d + EPS

    def make_k(self, i):
        e = self.get("e", i)
        return (4.0 / 3.0) * (e * e)

    def make_x(self, i):
        return self.get("e", i) * self.get("d", i)

    def make_q(self, i):
        return self.get("k", i) + self.get("p", i)

    def make_l(self, i):
        s = self.get("k", i) + self.get("e", i) * self.get("d", i + 1) + self.get("p", i + 1)
        return s * s

    def make_m(self, i):
        s = self.get("q", i) + self.get("x", i)
        return s * s

    def make_r(self, i):
        s = self.get("q", i) - self.get("x", i)
        return s * s


def correction(s0, s1, s2, t0, t2):
    a = 3.0 * s0
    r2 = s2 + s2
    total = s1 * s2 + a * (r2 + s1)
    return (s1 * (1.0 / total)) * (r2 * t0 + a * t2)


def interface(plus, minus, i):
    cp = correction(
        plus.get("l", i - 2), plus.get("m", i - 1), plus.get("r", i),
        plus.get("t", i - 2), plus.get("t", i - 1),
    )
    cm = correction(
        minus.get("r", i + 1), minus.get("m", i), minus.get("l", i - 1),
        minus.get("t", i), minus.get("t", i - 1),
    )
    near = plus.get("d", i) - minus.get("d", i)
    far = plus.get("d", i - 1) - minus.get("d", i + 1)
    return (plus.g(i) + minus.g(i + 1)) + (1.0 / 6.0) * ((near + near) + far + (cm - cp))


def pick(index, values):
    out = jnp.float32(values[-1])
    for k in range(len(values) - 2, -1, -1):
        out = jnp.where(index == k, jnp.float32(values[k]), out)
    return out


def kernel(
    sizes, init_hbm, guess_hbm, out_hbm,
    w, fx, fy, fz, gs, hs, hx, rate, r1, s2, r2, init, stage,
    ysend, yrecv, fyp, part, amsg, ar1, amid, ar2, alpha,
    load_sem, out_sem, xs_sem, xr_sem, ys_sem, yr_sem,
    a1s_sem, a1r_sem, a2s_sem, a2r_sem, e1s_sem, e1r_sem, e2s_sem, e2r_sem,
):
    n_gx, n_gy = sizes
    n_z, n_y = n_gx // 2, 2 * n_gy
    node, gx, gy = lax.axis_index("node"), lax.axis_index("gx"), lax.axis_index("gy")
    mate_a = node + 1 - 2 * lax.rem(node, 2)
    mate_b = 3 - node
    z, hi = gx // 2, lax.rem(gx, 2)
    y = hi * n_gy + gy

    def y_peer(step):
        other = lax.rem(y + step, n_y)
        return {"gx": z * 2 + other // n_gy, "gy": lax.rem(other, n_gy)}

    def z_peer(step):
        return {"gx": lax.rem(z + step, n_z) * 2 + hi}

    up_x = {"gx": lax.rem(gx + 1, n_gx)}
    down_x = {"gx": lax.rem(gx + n_gx - 1, n_gx)}
    up_y = {"gy": lax.rem(gy + 1, n_gy)}
    down_y = {"gy": lax.rem(gy + n_gy - 1, n_gy)}
    first_mates = ({"node": mate_a}, {"node": mate_b})
    second_mates = ({"node": mate_b}, {"node": mate_a})

    load_init = pltpu.make_async_copy(init_hbm, init, load_sem.at[0])
    load_guess = pltpu.make_async_copy(guess_hbm.at[0], stage, load_sem.at[1])
    load_guess.start()
    load_init.start()

    barrier = pltpu.get_barrier_semaphore()
    greeted = [y_peer(k) for k in range(1, n_y)] + [z_peer(k) for k in range(1, n_z)]
    greeted += [up_x, down_x, {"node": mate_a}, {"node": mate_b}]
    for peer in greeted:
        pl.semaphore_signal(barrier, inc=1, device_id=peer, device_id_type=MESH)

    def entry(f):
        return pick(node, [0.5 * step_size * f(m, m + 1 - 2 * (m % 2), 3 - m) for m in range(4)])

    table = radau_weights
    own = entry(lambda m, a, b: table[m][m])
    got = (entry(lambda m, a, b: table[m][a]), entry(lambda m, a, b: table[m][b]))
    give_own = (entry(lambda m, a, b: table[b][m]), entry(lambda m, a, b: table[a][m]))
    give_got = (entry(lambda m, a, b: table[b][a]), entry(lambda m, a, b: table[a][b]))

    lane = lax.broadcasted_iota(jnp.int32, (1, LANES), 1)

    def rows(h):
        return slice(8 + 8 * h, 16 + 8 * h)

    def half(h):
        return slice(8 * h, 8 * h + 8)

    def take_plane(s, p, fields):
        best = [part[k] for k in range(3)]
        for h in range(2):
            u = fields[h]
            inverse, velocity, pressure = primitives(u)
            sound = jnp.sqrt(heat_ratio * pressure * inverse)
            for k in range(3):
                best[k] = jnp.maximum(best[k], jnp.abs(velocity[k]) + sound)
            f0, f1, f2 = (flux(u, velocity, pressure, k) for k in range(3))
            for c in range(5):
                w[s, c, p + 3, rows(h), :] = u[c]
                fx[c, p + 3, half(h), :] = f0[c]
                fy[c, p, rows(h), :] = f1[c]
                fz[c, p, half(h), :] = f2[c]
        for k in range(3):
            part[k] = best[k]

    for k in range(3):
        part[k] = jnp.zeros((8, LANES), jnp.float32)
    load_guess.wait()

    def first(p, _):
        take_plane(0, p, [[stage[c, p, half(h), :] * SCALE for c in range(5)] for h in range(2)])
        return 0

    lax.fori_loop(0, NX, first, 0)
    load_init.wait()
    pl.semaphore_wait(barrier, len(greeted))

    def x_halo(s):
        low = pltpu.make_async_remote_copy(
            src_ref=w.at[s, :, pl.ds(3, 3), pl.ds(8, 16), :], dst_ref=w.at[s, :, pl.ds(15, 3), pl.ds(8, 16), :],
            send_sem=xs_sem.at[0], recv_sem=xr_sem.at[s, 0], device_id=down_x, device_id_type=MESH)
        high = pltpu.make_async_remote_copy(
            src_ref=w.at[s, :, pl.ds(12, 3), pl.ds(8, 16), :], dst_ref=w.at[s, :, pl.ds(0, 3), pl.ds(8, 16), :],
            send_sem=xs_sem.at[1], recv_sem=xr_sem.at[s, 1], device_id=up_x, device_id_type=MESH)
        return low, high

    def y_halo(s):
        low = pltpu.make_async_remote_copy(
            src_ref=ysend.at[0], dst_ref=yrecv.at[s, 1],
            send_sem=ys_sem.at[0], recv_sem=yr_sem.at[s, 1], device_id=down_y, device_id_type=MESH)
        high = pltpu.make_async_remote_copy(
            src_ref=ysend.at[1], dst_ref=yrecv.at[s, 0],
            send_sem=ys_sem.at[1], recv_sem=yr_sem.at[s, 0], device_id=up_y, device_id_type=MESH)
        return low, high

    def swap(s, h, chunk, second):
        start, count = CHUNKS[chunk]
        span = pl.ds(start, count)
        return pltpu.make_async_remote_copy(
            src_ref=(s2 if second else rate).at[h, span], dst_ref=(r2 if second else r1).at[s, h, span],
            send_sem=(e2s_sem if second else e1s_sem).at[h, chunk],
            recv_sem=(e2r_sem if second else e1r_sem).at[s, h, chunk],
            device_id=(second_mates if second else first_mates)[h], device_id_type=MESH)

    def x_pass(s, cells, faces, planes, saved_in, saved_out, add):
        def body(c, _):
            a = alpha[0]
            for h in range(2):
                up, down = {}, {}
                for i in cells:
                    f = fx[c, i, half(h), :]
                    au = a * w[s, c, i, rows(h), :]
                    up[i] = f + au
                    down[i] = f - au
                up, down = Line(up), Line(down)
                flows = {}
                for i, slot in saved_in:
                    flows[i] = hx[slot, h, c]
                for i in faces:
                    flows[i] = interface(up, down, i - 1)
                for i, slot in saved_out:
                    hx[slot, h, c] = flows[i]
                for i in planes:
                    along_x = flows[i] - flows[i + 1]
                    rate[h, i - 3, c] = rate[h, i - 3, c] + along_x if add else along_x
            return 0

        lax.fori_loop(0, 5, body, 0)

    def yz_plane(s, p, add):
        a1 = alpha[1]
        a2 = alpha[2]
        for c in range(5):
            for j in range(4):
                tile = slice(8 * j, 8 * j + 8)
                f = fy[c, p, tile, :]
                au = a1 * w[s, c, p + 3, tile, :]
                gs[0, c, tile, :] = f + au
                gs[1, c, tile, :] = f - au
        for c in range(5):
            for j in range(3):
                base = 8 + 8 * j
                up = Line({i: gs[0, c, base - 1 + i : base + 7 + i, :] for i in range(-2, 3)})
                down = Line({i: gs[1, c, base - 1 + i : base + 7 + i, :] for i in range(-1, 4)})
                hs[c, 8 * j : 8 * j + 8, :] = interface(up, down, 0)
        for c in range(5):
            for h in range(2):
                f = fz[c, p, half(h), :]
                au = a2 * w[s, c, p + 3, rows(h), :]
                right, left = f + au, f - au
                up = Line({i: right if i == 0 else pltpu.roll(right, (-i) % LANES, 1) for i in range(-2, 3)})
                down = Line({i: left if i == 0 else pltpu.roll(left, (-i) % LANES, 1) for i in range(-1, 4)})
                flow = interface(up, down, 0)
                along_z = pltpu.roll(flow, 1, 1) - flow
                along_y = hs[c, half(h), :] - hs[c, 8 * h + 1 : 8 * h + 9, :]
                along = along_y + along_z
                rate[h, p, c] = rate[h, p, c] + along if add else along

    def combine(s, chunk):
        start, count = CHUNKS[chunk]
        for h in range(2):
            swap(s, h, chunk, False).wait_recv()

            def body(p, _, h=h):
                for c in range(5):
                    s2[h, p, c] = give_own[h] * rate[h, p, c] + give_got[h] * r1[s, h, p, c]
                return 0

            lax.fori_loop(start, start + count, body, 0)
            swap(s, h, chunk, True).start()

    def finish(s, chunk):
        start, count = CHUNKS[chunk]
        for h in range(2):
            swap(s, h, chunk, True).wait_recv()

        def updated(p):
            return [
                [
                    init[c, p, half(h), :] * SCALE
                    + (own * rate[h, p, c] + (got[h] * r1[s, h, p, c] + r2[s, h, p, c]))
                    for c in range(5)
                ]
                for h in range(2)
            ]

        @pl.when(s < SWEEPS - 1)
        def _():
            def body(p, _):
                take_plane(s + 1, p, updated(p))
                return 0

            lax.fori_loop(start, start + count, body, 0)

        @pl.when(s == SWEEPS - 1)
        def _():
            def body(p, _):
                fields = updated(p)
                for h in range(2):
                    for c in range(5):
                        stage[c, p, half(h), :] = fields[h][c] * (1.0 / SCALE)
                return 0

            lax.fori_loop(start, start + count, body, 0)

    def whole(ref, sem):
        return pltpu.make_async_copy(ref, ref, sem)

    def sweep(s, _):
        tops = [jnp.max(part[k], axis=(0, 1), keepdims=True) for k in range(3)]
        amsg[...] = jnp.where(lane < 43, tops[0], jnp.where(lane < 86, tops[1], tops[2]))
        for k in range(1, n_y):
            pltpu.make_async_remote_copy(
                src_ref=amsg, dst_ref=ar1.at[s, k - 1], send_sem=a1s_sem, recv_sem=a1r_sem.at[s],
                device_id=y_peer(k), device_id_type=MESH).start()
        for c in range(5):
            for p in range(NX):
                ysend[0, c, 3 * p : 3 * p + 3, :] = w[s, c, p + 3, 8:11, :]
                ysend[1, c, 3 * p : 3 * p + 3, :] = w[s, c, p + 3, 21:24, :]
        for copy in y_halo(s):
            copy.start()
        whole(ar1.at[s], a1r_sem.at[s]).wait()
        for copy in x_halo(s):
            copy.start()
        best = amsg[...]
        for k in range(n_y - 1):
            best = jnp.maximum(best, ar1[s, k])
        amid[...] = best
        for k in range(1, n_z):
            pltpu.make_async_remote_copy(
                src_ref=amid, dst_ref=ar2.at[s, k - 1], send_sem=a2s_sem, recv_sem=a2r_sem.at[s],
                device_id=z_peer(k), device_id_type=MESH).start()

        for side, copy in ((1, y_halo(s)[0]), (0, y_halo(s)[1])):
            copy.wait_recv()
            for j in range(5):
                tile = slice(8 * j, 8 * j + 8)
                u = [yrecv[s, side, c, tile, :] for c in range(5)]
                _, velocity, pressure = primitives(u)
                parts = flux(u, velocity, pressure, 1)
                for c in range(5):
                    fyp[side, c, tile, :] = parts[c]
            at = slice(5, 8) if side == 0 else slice(24, 27)
            for c in range(5):
                for p in range(NX):
                    w[s, c, p + 3, at, :] = yrecv[s, side, c, 3 * p : 3 * p + 3, :]
                    fy[c, p, at, :] = fyp[side, c, 3 * p : 3 * p + 3, :]

        if n_z > 1:
            whole(ar2.at[s], a2r_sem.at[s]).wait()
            best = amid[...]
            for k in range(n_z - 1):
                best = jnp.maximum(best, ar2[s, k])
        bounds = (0, 43, 86, LANES)
        for k in range(3):
            mine = jnp.where((lane >= bounds[k]) & (lane < bounds[k + 1]), best, 0.0)
            alpha[k] = jnp.broadcast_to(jnp.max(mine, axis=1, keepdims=True), (8, LANES))
            part[k] = jnp.zeros((8, LANES), jnp.float32)

        def run(chunk, add):
            start, count = CHUNKS[chunk]

            def body(p, _):
                yz_plane(s, p, add)
                return 0

            lax.fori_loop(start, start + count, body, 0)

        def send(chunk):
            for h in range(2):
                swap(s, h, chunk, False).start()

        def halo_planes(first):
            def body(i, _):
                for h in range(2):
                    u = [w[s, c, i, rows(h), :] for c in range(5)]
                    _, velocity, pressure = primitives(u)
                    parts = flux(u, velocity, pressure, 0)
                    for c in range(5):
                        fx[c, i, half(h), :] = parts[c]
                return 0

            lax.fori_loop(first, first + 3, body, 0)

        to_low, to_high = x_halo(s)
        x_pass(s, range(3, 15), range(6, 13), range(6, 12), (), ((6, 0), (12, 1)), False)
        run(0, True)
        send(0)
        run(1, True)
        send(1)
        run(2, False)
        combine(s, 0)
        to_low.wait_recv()
        halo_planes(15)
        x_pass(s, range(10, 18), range(13, 16), range(12, 15), ((12, 1),), (), False)
        run(3, True)
        send(3)
        combine(s, 1)
        to_high.wait_recv()
        halo_planes(0)
        x_pass(s, range(0, 8), range(3, 6), range(3, 6), ((6, 0),), (), True)
        send(2)
        to_low.wait_send()
        to_high.wait_send()
        for copy in y_halo(s):
            copy.wait_send()
        whole(ar1.at[s], a1s_sem).wait()
        if n_z > 1:
            whole(ar2.at[s], a2s_sem).wait()
        finish(s, 0)
        combine(s, 3)
        finish(s, 1)
        combine(s, 2)
        finish(s, 3)
        finish(s, 2)
        for chunk in range(len(CHUNKS)):
            for h in range(2):
                swap(s, h, chunk, False).wait_send()
                swap(s, h, chunk, True).wait_send()
        return 0

    lax.fori_loop(0, SWEEPS, sweep, 0)
    store = pltpu.make_async_copy(stage, out_hbm.at[0], out_sem)
    store.start()
    store.wait()


def call(sizes, initial, guesses):
    n_z, n_y = sizes[0] // 2, 2 * sizes[1]
    f32 = jnp.float32
    dma = pltpu.SemaphoreType.DMA
    chunks = len(CHUNKS)
    tile = (8, LANES)

    def vm(*shape):
        return pltpu.VMEM(shape, f32)

    return pl.pallas_call(
        functools.partial(kernel, sizes),
        out_shape=jax.ShapeDtypeStruct(guesses.shape, f32),
        in_specs=[pl.BlockSpec(memory_space=pl.ANY)] * 2,
        out_specs=pl.BlockSpec(memory_space=pl.ANY),
        scratch_shapes=[
            vm(SWEEPS, 5, NX + 6, 32, LANES),
            vm(5, NX + 6, NY, LANES),
            vm(5, NX, 32, LANES),
            vm(5, NX, NY, LANES),
            vm(2, 5, 40, LANES),
            vm(5, 24, LANES),
            vm(2, 2, 5, *tile),
            vm(2, NX, 5, *tile),
            vm(SWEEPS, 2, NX, 5, *tile),
            vm(2, NX, 5, *tile),
            vm(SWEEPS, 2, NX, 5, *tile),
            vm(5, NX, NY, LANES),
            vm(5, NX, NY, LANES),
            vm(2, 5, YROWS, LANES),
            vm(SWEEPS, 2, 5, YROWS, LANES),
            vm(2, 5, YROWS, LANES),
            vm(3, *tile),
            vm(1, LANES),
            vm(SWEEPS, n_y - 1, 1, LANES),
            vm(1, LANES),
            vm(SWEEPS, max(n_z - 1, 1), 1, LANES),
            vm(3, *tile),
            dma((2,)), dma,
            dma((2,)), dma((SWEEPS, 2)), dma((2,)), dma((SWEEPS, 2)),
            dma, dma((SWEEPS,)), dma, dma((SWEEPS,)),
            dma((2, chunks)), dma((SWEEPS, 2, chunks)), dma((2, chunks)), dma((SWEEPS, 2, chunks)),
        ],
        compiler_params=pltpu.CompilerParams(
            collective_id=0, has_side_effects=True, vmem_limit_bytes=60 << 20
        ),
    )(initial, guesses)


def solution(mesh):
    sizes = (mesh.shape["gx"], mesh.shape["gy"])
    placed = (P(None, "gx", "gy", None), P("node", None, "gx", "gy", None))
    return jax.shard_map(
        functools.partial(call, sizes),
        mesh=mesh,
        in_specs=placed,
        out_specs=P("node", None, "gx", "gy", None),
        check_vma=False,
    )
```

```python
import functools

import jax
import jax.numpy as jnp
from jax import lax
from jax.experimental import pallas as pl
from jax.experimental.pallas import tpu as pltpu
from jax.sharding import PartitionSpec as P

SWEEPS = 2
SCALE = 1.0 / 64.0

heat_ratio = 1.4
step_size = 0.025
density_floor = 0.5
pressure_floor = 0.25
epsilon = 1e-06
radau_weights = [
    [0.112999479323156, -0.040309220723522, 0.025802377420336, -0.009904676507266],
    [0.2343839957474, 0.206892573935359, -0.047857128048541, 0.016047422806516],
    [0.21668178462325, 0.406123263867373, 0.189036518170056, -0.024182104899833],
    [0.220462211176768, 0.388193468843172, 0.32884431998006, 0.0625],
]
MESH = pl.DeviceIdType.MESH
EPS = epsilon * 4.0 * SCALE * SCALE
NX, NY, LANES = 12, 16, 128
CHUNKS = ((3, 2), (5, 2), (7, 2), (9, 3), (0, 2), (2, 1))
YROWS = 40


def primitives(u):
    density = jnp.maximum(u[0], density_floor * SCALE)
    inverse = 1.0 / density
    velocity = [u[k] * inverse for k in (1, 2, 3)]
    kinetic = u[1] * velocity[0] + u[2] * velocity[1] + u[3] * velocity[2]
    pressure = jnp.maximum(0.4 * (u[4] - 0.5 * kinetic), pressure_floor * SCALE)
    return inverse, velocity, pressure


def flux(u, velocity, pressure, k):
    speed = velocity[k]
    parts = [u[k + 1], u[1] * speed, u[2] * speed, u[3] * speed, (u[4] + pressure) * speed]
    parts[k + 1] = parts[k + 1] + pressure
    return parts


class Line:
    def __init__(self, cells):
        self.cells = cells
        self.made = {}

    def get(self, name, i):
        key = (name, i)
        if key not in self.made:
            self.made[key] = getattr(self, "make_" + name)(i)
        return self.made[key]

    def g(self, i):
        return self.cells[i]

    def make_d(self, i):
        return self.cells[i + 1] - self.cells[i]

    def make_e(self, i):
        return self.get("d", i + 1) - self.get("d", i)

    def make_t(self, i):
        return self.get("e", i + 1) - self.get("e", i)

    def make_p(self, i):
        d = self.get("d", i)
        return d * d + EPS

    def make_k(self, i):
        e = self.get("e", i)
        return (4.0 / 3.0) * (e * e)

    def make_x(self, i):
        return self.get("e", i) * self.get("d", i)

    def make_q(self, i):
        return self.get("k", i) + self.get("p", i)

    def make_l(self, i):
        s = self.get("k", i) + self.get("e", i) * self.get("d", i + 1) + self.get("p", i + 1)
        return s * s

    def make_m(self, i):
        s = self.get("q", i) + self.get("x", i)
        return s * s

    def make_r(self, i):
        s = self.get("q", i) - self.get("x", i)
        return s * s


def correction(s0, s1, s2, t0, t2):
    a = 3.0 * s0
    r2 = s2 + s2
    total = s1 * s2 + a * (r2 + s1)
    return (s1 * (1.0 / total)) * (r2 * t0 + a * t2)


def interface(plus, minus, i):
    cp = correction(
        plus.get("l", i - 2), plus.get("m", i - 1), plus.get("r", i),
        plus.get("t", i - 2), plus.get("t", i - 1),
    )
    cm = correction(
        minus.get("r", i + 1), minus.get("m", i), minus.get("l", i - 1),
        minus.get("t", i), minus.get("t", i - 1),
    )
    near = plus.get("d", i) - minus.get("d", i)
    far = plus.get("d", i - 1) - minus.get("d", i + 1)
    return (plus.g(i) + minus.g(i + 1)) + (1.0 / 6.0) * ((near + near) + far + (cm - cp))


def pick(index, values):
    out = jnp.float32(values[-1])
    for k in range(len(values) - 2, -1, -1):
        out = jnp.where(index == k, jnp.float32(values[k]), out)
    return out


def kernel(
    sizes, init_hbm, guess_hbm, out_hbm,
    w, fx, fy, fz, gs, hs, hx, rate, r1, s2, r2, init, stage,
    ysend, yrecv, fyp, part, amsg, ar1, amid, ar2, alpha,
    load_sem, out_sem, xs_sem, xr_sem, ys_sem, yr_sem,
    a1s_sem, a1r_sem, a2s_sem, a2r_sem, e1s_sem, e1r_sem, e2s_sem, e2r_sem,
):
    n_gx, n_gy = sizes
    n_z, n_y = n_gx // 2, 2 * n_gy
    node, gx, gy = lax.axis_index("node"), lax.axis_index("gx"), lax.axis_index("gy")
    mate_a = node + 1 - 2 * lax.rem(node, 2)
    mate_b = 3 - node
    z, hi = gx // 2, lax.rem(gx, 2)
    y = hi * n_gy + gy

    def y_peer(step):
        other = lax.rem(y + step, n_y)
        return {"gx": z * 2 + other // n_gy, "gy": lax.rem(other, n_gy)}

    def z_peer(step):
        return {"gx": lax.rem(z + step, n_z) * 2 + hi}

    up_x = {"gx": lax.rem(gx + 1, n_gx)}
    down_x = {"gx": lax.rem(gx + n_gx - 1, n_gx)}
    up_y = {"gy": lax.rem(gy + 1, n_gy)}
    down_y = {"gy": lax.rem(gy + n_gy - 1, n_gy)}
    first_mates = ({"node": mate_a}, {"node": mate_b})
    second_mates = ({"node": mate_b}, {"node": mate_a})

    load_init = pltpu.make_async_copy(init_hbm, init, load_sem.at[0])
    load_guess = pltpu.make_async_copy(guess_hbm.at[0], stage, load_sem.at[1])
    load_guess.start()
    load_init.start()

    barrier = pltpu.get_barrier_semaphore()
    greeted = [y_peer(k) for k in range(1, n_y)] + [z_peer(k) for k in range(1, n_z)]
    greeted += [up_x, down_x, {"node": mate_a}, {"node": mate_b}]
    for peer in greeted:
        pl.semaphore_signal(barrier, inc=1, device_id=peer, device_id_type=MESH)

    def entry(f):
        return pick(node, [0.5 * step_size * f(m, m + 1 - 2 * (m % 2), 3 - m) for m in range(4)])

    table = radau_weights
    own = entry(lambda m, a, b: table[m][m])
    got = (entry(lambda m, a, b: table[m][a]), entry(lambda m, a, b: table[m][b]))
    give_own = (entry(lambda m, a, b: table[b][m]), entry(lambda m, a, b: table[a][m]))
    give_got = (entry(lambda m, a, b: table[b][a]), entry(lambda m, a, b: table[a][b]))

    lane = lax.broadcasted_iota(jnp.int32, (1, LANES), 1)

    def rows(h):
        return slice(8 + 8 * h, 16 + 8 * h)

    def half(h):
        return slice(8 * h, 8 * h + 8)

    def take_plane(s, p, fields):
        best = [part[k] for k in range(3)]
        for h in range(2):
            u = fields[h]
            inverse, velocity, pressure = primitives(u)
            sound = jnp.sqrt(heat_ratio * pressure * inverse)
            for k in range(3):
                best[k] = jnp.maximum(best[k], jnp.abs(velocity[k]) + sound)
            f0, f1, f2 = (flux(u, velocity, pressure, k) for k in range(3))
            for c in range(5):
                w[s, c, p + 3, rows(h), :] = u[c]
                fx[c, p + 3, half(h), :] = f0[c]
                fy[c, p, rows(h), :] = f1[c]
                fz[c, p, half(h), :] = f2[c]
        for k in range(3):
            part[k] = best[k]

    for k in range(3):
        part[k] = jnp.zeros((8, LANES), jnp.float32)
    load_guess.wait()

    def first(p, _):
        take_plane(0, p, [[stage[c, p, half(h), :] * SCALE for c in range(5)] for h in range(2)])
        return 0

    lax.fori_loop(0, NX, first, 0)
    load_init.wait()
    pl.semaphore_wait(barrier, len(greeted))

    def x_halo(s):
        low = pltpu.make_async_remote_copy(
            src_ref=w.at[s, :, pl.ds(3, 3), pl.ds(8, 16), :], dst_ref=w.at[s, :, pl.ds(15, 3), pl.ds(8, 16), :],
            send_sem=xs_sem.at[0], recv_sem=xr_sem.at[s, 0], device_id=down_x, device_id_type=MESH)
        high = pltpu.make_async_remote_copy(
            src_ref=w.at[s, :, pl.ds(12, 3), pl.ds(8, 16), :], dst_ref=w.at[s, :, pl.ds(0, 3), pl.ds(8, 16), :],
            send_sem=xs_sem.at[1], recv_sem=xr_sem.at[s, 1], device_id=up_x, device_id_type=MESH)
        return low, high

    def y_halo(s):
        low = pltpu.make_async_remote_copy(
            src_ref=ysend.at[0], dst_ref=yrecv.at[s, 1],
            send_sem=ys_sem.at[0], recv_sem=yr_sem.at[s, 1], device_id=down_y, device_id_type=MESH)
        high = pltpu.make_async_remote_copy(
            src_ref=ysend.at[1], dst_ref=yrecv.at[s, 0],
            send_sem=ys_sem.at[1], recv_sem=yr_sem.at[s, 0], device_id=up_y, device_id_type=MESH)
        return low, high

    def swap(s, h, chunk, second):
        start, count = CHUNKS[chunk]
        span = pl.ds(start, count)
        return pltpu.make_async_remote_copy(
            src_ref=(s2 if second else rate).at[h, span], dst_ref=(r2 if second else r1).at[s, h, span],
            send_sem=(e2s_sem if second else e1s_sem).at[h, chunk],
            recv_sem=(e2r_sem if second else e1r_sem).at[s, h, chunk],
            device_id=(second_mates if second else first_mates)[h], device_id_type=MESH)

    def x_pass(s, cells, faces, planes, saved_in, saved_out, add):
        def body(c, _):
            a = alpha[0]
            for h in range(2):
                up, down = {}, {}
                for i in cells:
                    f = fx[c, i, half(h), :]
                    au = a * w[s, c, i, rows(h), :]
                    up[i] = f + au
                    down[i] = f - au
                up, down = Line(up), Line(down)
                flows = {}
                for i, slot in saved_in:
                    flows[i] = hx[slot, h, c]
                for i in faces:
                    flows[i] = interface(up, down, i - 1)
                for i, slot in saved_out:
                    hx[slot, h, c] = flows[i]
                for i in planes:
                    along_x = flows[i] - flows[i + 1]
                    rate[h, i - 3, c] = rate[h, i - 3, c] + along_x if add else along_x
            return 0

        lax.fori_loop(0, 5, body, 0)

    def yz_plane(s, p, add):
        a1 = alpha[1]
        a2 = alpha[2]
        for c in range(5):
            for j in range(4):
                tile = slice(8 * j, 8 * j + 8)
                f = fy[c, p, tile, :]
                au = a1 * w[s, c, p + 3, tile, :]
                gs[0, slice(40 * c + 8 * j, 40 * c + 8 * j + 8), :] = f + au
                gs[1, slice(40 * c + 8 * j, 40 * c + 8 * j + 8), :] = f - au
        for c in range(5):
            for j in range(2):
                base = 40 * c + 8 + 8 * j
                up = Line({i: gs[0, base - 1 + i : base + 7 + i, :] for i in range(-2, 3)})
                down = Line({i: gs[1, base - 1 + i : base + 7 + i, :] for i in range(-1, 4)})
                hs[24 * c + 8 * j : 24 * c + 8 * j + 8, :] = interface(up, down, 0)
        up = Line({i: gs[0, pl.ds(23 + i, 8, stride=40), :] for i in range(-2, 3)})
        down = Line({i: gs[1, pl.ds(23 + i, 8, stride=40), :] for i in range(-1, 4)})
        hs[pl.ds(16, 8, stride=24), :] = interface(up, down, 0)
        for c in range(5):
            for h in range(2):
                f = fz[c, p, half(h), :]
                au = a2 * w[s, c, p + 3, rows(h), :]
                right, left = f + au, f - au
                up = Line({i: right if i == 0 else pltpu.roll(right, (-i) % LANES, 1) for i in range(-2, 3)})
                down = Line({i: left if i == 0 else pltpu.roll(left, (-i) % LANES, 1) for i in range(-1, 4)})
                flow = interface(up, down, 0)
                along_z = pltpu.roll(flow, 1, 1) - flow
                row = 24 * c + 8 * h
                along_y = hs[row : row + 8, :] - hs[row + 1 : row + 9, :]
                along = along_y + along_z
                rate[h, p, c] = rate[h, p, c] + along if add else along

    def combine(s, chunk):
        start, count = CHUNKS[chunk]
        for h in range(2):
            swap(s, h, chunk, False).wait_recv()

            def body(p, _, h=h):
                for c in range(5):
                    s2[h, p, c] = give_own[h] * rate[h, p, c] + give_got[h] * r1[s, h, p, c]
                return 0

            lax.fori_loop(start, start + count, body, 0)
            swap(s, h, chunk, True).start()

    def finish(s, chunk):
        start, count = CHUNKS[chunk]
        for h in range(2):
            swap(s, h, chunk, True).wait_recv()

        def updated(p):
            return [
                [
                    init[c, p, half(h), :] * SCALE
                    + (own * rate[h, p, c] + (got[h] * r1[s, h, p, c] + r2[s, h, p, c]))
                    for c in range(5)
                ]
                for h in range(2)
            ]

        @pl.when(s < SWEEPS - 1)
        def _():
            def body(p, _):
                take_plane(s + 1, p, updated(p))
                return 0

            lax.fori_loop(start, start + count, body, 0)

        @pl.when(s == SWEEPS - 1)
        def _():
            def body(p, _):
                fields = updated(p)
                for h in range(2):
                    for c in range(5):
                        stage[c, p, half(h), :] = fields[h][c]
                return 0

            lax.fori_loop(start, start + count, body, 0)
            store(chunk).start()

    def store(chunk):
        span = pl.ds(*CHUNKS[chunk])
        return pltpu.make_async_copy(stage.at[:, span], out_hbm.at[0, :, span], out_sem.at[chunk])

    def whole(ref, sem):
        return pltpu.make_async_copy(ref, ref, sem)

    def sweep(s, _):
        tops = [jnp.max(part[k], axis=(0, 1), keepdims=True) for k in range(3)]
        amsg[...] = jnp.where(lane < 43, tops[0], jnp.where(lane < 86, tops[1], tops[2]))
        for k in range(1, n_y):
            pltpu.make_async_remote_copy(
                src_ref=amsg, dst_ref=ar1.at[s, k - 1], send_sem=a1s_sem, recv_sem=a1r_sem.at[s],
                device_id=y_peer(k), device_id_type=MESH).start()
        for c in range(5):
            for p in range(NX):
                ysend[0, c, 3 * p : 3 * p + 3, :] = w[s, c, p + 3, 8:11, :]
                ysend[1, c, 3 * p : 3 * p + 3, :] = w[s, c, p + 3, 21:24, :]
        for copy in y_halo(s):
            copy.start()
        whole(ar1.at[s], a1r_sem.at[s]).wait()
        for copy in x_halo(s):
            copy.start()
        best = amsg[...]
        for k in range(n_y - 1):
            best = jnp.maximum(best, ar1[s, k])
        amid[...] = best
        for k in range(1, n_z):
            pltpu.make_async_remote_copy(
                src_ref=amid, dst_ref=ar2.at[s, k - 1], send_sem=a2s_sem, recv_sem=a2r_sem.at[s],
                device_id=z_peer(k), device_id_type=MESH).start()

        for side, copy in ((1, y_halo(s)[0]), (0, y_halo(s)[1])):
            copy.wait_recv()
            for j in range(5):
                tile = slice(8 * j, 8 * j + 8)
                u = [yrecv[s, side, c, tile, :] for c in range(5)]
                _, velocity, pressure = primitives(u)
                parts = flux(u, velocity, pressure, 1)
                for c in range(5):
                    fyp[side, c, tile, :] = parts[c]
            at = slice(5, 8) if side == 0 else slice(24, 27)
            for c in range(5):
                for p in range(NX):
                    w[s, c, p + 3, at, :] = yrecv[s, side, c, 3 * p : 3 * p + 3, :]
                    fy[c, p, at, :] = fyp[side, c, 3 * p : 3 * p + 3, :]

        if n_z > 1:
            whole(ar2.at[s], a2r_sem.at[s]).wait()
            best = amid[...]
            for k in range(n_z - 1):
                best = jnp.maximum(best, ar2[s, k])
        bounds = (0, 43, 86, LANES)
        for k in range(3):
            mine = jnp.where((lane >= bounds[k]) & (lane < bounds[k + 1]), best, 0.0)
            alpha[k] = jnp.broadcast_to(jnp.max(mine, axis=1, keepdims=True), (8, LANES))
            part[k] = jnp.zeros((8, LANES), jnp.float32)

        def run(start, count, add):
            def body(p, _):
                yz_plane(s, p, add)
                return 0

            lax.fori_loop(start, start + count, body, 0)

        def send(chunk):
            for h in range(2):
                swap(s, h, chunk, False).start()

        def halo_planes(first):
            def body(i, _):
                for h in range(2):
                    u = [w[s, c, i, rows(h), :] for c in range(5)]
                    _, velocity, pressure = primitives(u)
                    parts = flux(u, velocity, pressure, 0)
                    for c in range(5):
                        fx[c, i, half(h), :] = parts[c]
                return 0

            lax.fori_loop(first, first + 3, body, 0)

        to_low, to_high = x_halo(s)
        x_pass(s, range(3, 15), range(6, 13), range(6, 12), (), ((6, 0), (12, 1)), False)
        for chunk in range(3):
            run(*CHUNKS[chunk], True)
            send(chunk)
        combine(s, 0)
        run(0, 3, False)
        combine(s, 1)
        to_low.wait_recv()
        halo_planes(15)
        x_pass(s, range(10, 18), range(13, 16), range(12, 15), ((12, 1),), (), False)
        run(*CHUNKS[3], True)
        send(3)
        combine(s, 2)
        to_high.wait_recv()
        halo_planes(0)
        x_pass(s, range(0, 8), range(3, 6), range(3, 6), ((6, 0),), (), True)
        send(4)
        send(5)
        to_low.wait_send()
        to_high.wait_send()
        for copy in y_halo(s):
            copy.wait_send()
        whole(ar1.at[s], a1s_sem).wait()
        if n_z > 1:
            whole(ar2.at[s], a2s_sem).wait()
        finish(s, 0)
        finish(s, 1)
        combine(s, 3)
        finish(s, 2)
        combine(s, 4)
        combine(s, 5)
        finish(s, 3)
        finish(s, 4)
        finish(s, 5)
        for chunk in range(len(CHUNKS)):
            for h in range(2):
                swap(s, h, chunk, False).wait_send()
                swap(s, h, chunk, True).wait_send()
        return 0

    lax.fori_loop(0, SWEEPS, sweep, 0)
    for chunk in range(len(CHUNKS)):
        store(chunk).wait()


def call(sizes, initial, guesses):
    n_z, n_y = sizes[0] // 2, 2 * sizes[1]
    f32 = jnp.float32
    dma = pltpu.SemaphoreType.DMA
    chunks = len(CHUNKS)
    tile = (8, LANES)

    def vm(*shape):
        return pltpu.VMEM(shape, f32)

    scaled = pl.pallas_call(
        functools.partial(kernel, sizes),
        out_shape=jax.ShapeDtypeStruct(guesses.shape, f32),
        in_specs=[pl.BlockSpec(memory_space=pl.ANY)] * 2,
        out_specs=pl.BlockSpec(memory_space=pl.ANY),
        scratch_shapes=[
            vm(SWEEPS, 5, NX + 6, 32, LANES),
            vm(5, NX + 6, NY, LANES),
            vm(5, NX, 32, LANES),
            vm(5, NX, NY, LANES),
            vm(2, 8 * 40, LANES),
            vm(8 * 24, LANES),
            vm(2, 2, 5, *tile),
            vm(2, NX, 5, *tile),
            vm(SWEEPS, 2, NX, 5, *tile),
            vm(2, NX, 5, *tile),
            vm(SWEEPS, 2, NX, 5, *tile),
            vm(5, NX, NY, LANES),
            vm(5, NX, NY, LANES),
            vm(2, 5, YROWS, LANES),
            vm(SWEEPS, 2, 5, YROWS, LANES),
            vm(2, 5, YROWS, LANES),
            vm(3, *tile),
            vm(1, LANES),
            vm(SWEEPS, n_y - 1, 1, LANES),
            vm(1, LANES),
            vm(SWEEPS, max(n_z - 1, 1), 1, LANES),
            vm(3, *tile),
            dma((2,)), dma((chunks,)),
            dma((2,)), dma((SWEEPS, 2)), dma((2,)), dma((SWEEPS, 2)),
            dma, dma((SWEEPS,)), dma, dma((SWEEPS,)),
            dma((2, chunks)), dma((SWEEPS, 2, chunks)), dma((2, chunks)), dma((SWEEPS, 2, chunks)),
        ],
        compiler_params=pltpu.CompilerParams(
            collective_id=0, has_side_effects=True, vmem_limit_bytes=60 << 20
        ),
    )(initial, guesses)
    return scaled * (1.0 / SCALE)


def solution(mesh):
    sizes = (mesh.shape["gx"], mesh.shape["gy"])
    placed = (P(None, "gx", "gy", None), P("node", None, "gx", "gy", None))
    return jax.shard_map(
        functools.partial(call, sizes),
        mesh=mesh,
        in_specs=placed,
        out_specs=P("node", None, "gx", "gy", None),
        check_vma=False,
    )
```
